32 devices in a mesh: groups: 2 (over x), prompt: 8 (over z, y), resp: 2 (over core).
Axes of the slice: x: 2, y: 2, z: 4, core: 2. Of those that a mesh axis runs over, the one named last changes fastest.
Arguments:
- queries: bfloat16 [16, 512, 1024], P(('groups', 'prompt'), 'resp'), parts along dimension 0, may hold values from -4096 to 4096
- grad_out: bfloat16 [16, 512, 1024], P(('groups', 'prompt'), 'resp'), parts along dimension 0, may hold values from -48 to 48
- keys_resp: bfloat16 [16, 512, 128], P(('groups', 'prompt'), 'resp'), parts along dimension 0, may hold values from -6 to 6
- values_resp: bfloat16 [16, 512, 128], P(('groups', 'prompt'), 'resp'), parts along dimension 0, may hold values from -6 to 6
- keys_prefix: bfloat16 [1024, 128], P(('groups', 'prompt')), parts along dimension 0, may hold values from -32 to 32
- values_prefix: bfloat16 [1024, 128], P(('groups', 'prompt')), parts along dimension 0, may hold values from -6 to 6
- lengths: int32 [16], P(('groups', 'prompt')), parts along dimension 0, may hold values from 1 to 512, as said below
- block_plan: int32 [16, 4], P(('groups', 'prompt'), 'resp'), parts along dimension 0, may hold values from 0 to 3, as said below
Outputs:
- query_grads: float32 [16, 512, 1024], P(('groups', 'prompt'), 'resp'), parts along dimension 0
- prefix_keygrad: float32 [1024, 128], P(('groups', 'prompt', 'resp')), parts along dimension 0
- prefix_valgrad: float32 [1024, 128], P(('groups', 'prompt', 'resp')), parts along dimension 0
- reply_keygrad: float32 [16, 512, 128], P(('groups', 'prompt'), 'resp'), parts along dimension 0
- reply_valgrad: float32 [16, 512, 128], P(('groups', 'prompt'), 'resp'), parts along dimension 0
The draws below stay inside these ranges and needn't reach their ends.
There are 2 independent parts, one for each index of `groups`. The reference program is written for one: setup_inputs(seed, part) draws one part's arguments, and reference() takes and returns one part's arrays. A program takes and returns all parts, laid end to end along the dimension named above; each array names one. Nothing has to cross between parts.
Inputs may be any that keep to these rules, and one draw needn't show every extreme that they name: `lengths`: one response has exactly 512 live positions. `block_plan`: each row is a permutation of 0 to 3; for every m, blocks 2 * m and 2 * m + 1 stand in different halves of the row.
All inputs are finite; a program needn't handle non-finite values.
Results may differ from the reference program's by a relative error of at most 0.0029.
Values may be sent and summed in bfloat16 or wider, within the bound.
A program may use at most 64 MiB of HBM per device.

```python
import jax
import jax.numpy as jnp
from jax import lax

HEAD = 128
HEADS = 8
RBLK = 128
P_SIZE = 512
NRESP = 8
LMAX = 512
NBLK = 4


def prefix_draw(key):
    normal_draw = jnp.clip(jax.random.normal(jax.random.fold_in(key, 101), (P_SIZE, HEAD), jnp.float32), -5.0, 5.0)
    return normal_draw


def draw_keys_prefix(key, part):
    return prefix_draw(key).astype(jnp.bfloat16)


def draw_queries(key, part):
    normal_draw = jnp.clip(jax.random.normal(jax.random.fold_in(key, 201), (NRESP, LMAX, HEADS, HEAD), jnp.float32), -5.0, 5.0)
    return normal_draw.reshape(NRESP, LMAX, HEADS * HEAD).astype(jnp.bfloat16)


def draw_lengths(key, part):
    lengths_draw = jax.random.randint(jax.random.fold_in(key, 401), (NRESP,), 1, LMAX + 1, jnp.int32)
    longest = jax.random.randint(jax.random.fold_in(key, 402), (), 0, NRESP, jnp.int32)
    return jnp.where(jnp.arange(NRESP, dtype=jnp.int32) == longest, LMAX, lengths_draw).astype(jnp.int32)


def draw_block_plan(key, part):
    half_count = NBLK // 2
    coin_flip = jax.random.randint(jax.random.fold_in(key, 301), (NRESP, half_count), 0, 2, jnp.int32)
    pair_start = 2 * jnp.arange(half_count, dtype=jnp.int32)
    to_first = pair_start[None, :] + coin_flip
    to_second = pair_start[None, :] + 1 - coin_flip
    halves = jnp.stack([to_first, to_second], 1)
    subkeys = jax.random.split(jax.random.fold_in(key, 302), NRESP * 2)
    orders = jax.vmap(lambda subkey: jax.random.permutation(subkey, half_count))(subkeys).reshape(NRESP, 2, half_count)
    placed = jnp.take_along_axis(halves, orders.astype(jnp.int32), axis=2)
    return placed.reshape(NRESP, NBLK).astype(jnp.int32)


def shard_levels(key, dims, cuts, least, top_value):
    loudness = 1.0
    for dim, parts in cuts:
        draws = jax.random.uniform(jax.random.fold_in(jax.random.fold_in(key, 6), dim), (parts,), jnp.float32, least / len(cuts), top_value / len(cuts))
        loudness = loudness * jnp.repeat(jnp.exp(draws), dims[dim] // parts).reshape((-1,) + (1,) * (len(dims) - 1 - dim))
    return loudness


def noise(rng, extent, deviation, most, cuts=(), held_as=jnp.bfloat16):
    values = jax.random.normal(rng, extent, jnp.float32) * deviation
    if len(cuts) > 0:
        values = shard_levels(rng, extent, cuts, -0.22, 0.18) * values
    return jnp.clip(values, min=-most, max=most).astype(held_as)


def setup_inputs(seed: int = 0, part: int = 0) -> dict:
    arg_keys = jax.random.split(jax.random.key(seed), 9)
    part_keys = jax.random.split(jax.random.fold_in(arg_keys[8], part), 9)
    return {
        "queries": draw_queries(jax.random.fold_in(jax.random.fold_in(arg_keys[8], part), 71), part),
        "grad_out": noise(part_keys[1], (NRESP, LMAX, HEADS * HEAD), 8.0, 48.0, ((0, 8), (1, 2))),
        "keys_resp": noise(part_keys[2], (NRESP, LMAX, HEAD), 1.0, 6.0, ((0, 8), (1, 2))),
        "values_resp": noise(part_keys[3], (NRESP, LMAX, HEAD), 1.0, 6.0, ((0, 8), (1, 2))),
        "keys_prefix": draw_keys_prefix(jax.random.fold_in(jax.random.fold_in(arg_keys[8], part), 71), part),
        "values_prefix": noise(part_keys[5], (P_SIZE, HEAD), 1.0, 6.0, ((0, 8),)),
        "lengths": draw_lengths(jax.random.fold_in(jax.random.fold_in(arg_keys[8], part), 71), part),
        "block_plan": draw_block_plan(jax.random.fold_in(jax.random.fold_in(arg_keys[8], part), 71), part),
    }


def reference(queries, grad_out, keys_resp, values_resp, keys_prefix, values_prefix, lengths, block_plan):
    score_scale = HEAD ** -0.5
    prefix_keys = keys_prefix.astype(jnp.float32)
    prefix_values = values_prefix.astype(jnp.float32)
    key_index = jnp.arange(P_SIZE + LMAX, dtype=jnp.int32)
    relative = key_index - P_SIZE
    positions = jnp.arange(LMAX, dtype=jnp.int32)

    def per_response(totals, block_item):
        query_rows, grad_rows, reply_keys, reply_values, length = block_item
        all_keys = jnp.concatenate([prefix_keys, reply_keys.astype(jnp.float32)], 0)
        all_values = jnp.concatenate([prefix_values, reply_values.astype(jnp.float32)], 0)
        query_heads = query_rows.astype(jnp.float32).reshape(LMAX, HEADS, HEAD)
        live_rows = positions < length
        grad_heads = jnp.where(live_rows[:, None, None], grad_rows.astype(jnp.float32).reshape(LMAX, HEADS, HEAD), jnp.float32(0.0))
        visible = (key_index[None, :] < P_SIZE) | ((relative[None, :] <= positions[:, None]) & (relative[None, :] < length))
        scores = jnp.einsum('rhd,kd->rhk', query_heads, all_keys) * score_scale
        scores = jnp.where(visible[:, None, :], scores, -jnp.inf)
        row_max = jnp.max(scores, -1, keepdims=True)
        exponent = jnp.exp(scores - row_max)
        weights = exponent / jnp.sum(exponent, -1, keepdims=True)
        grad_weight = jnp.einsum('rhd,kd->rhk', grad_heads, all_values)
        row_inner = jnp.sum(weights * grad_weight, -1, keepdims=True)
        grad_score = lax.optimization_barrier((weights * (grad_weight - row_inner)).astype(jnp.bfloat16)).astype(jnp.float32)
        rounded_weights = lax.optimization_barrier(weights.astype(jnp.bfloat16)).astype(jnp.float32)
        grad_q = jnp.einsum('rhk,kd->rhd', grad_score, all_keys) * score_scale
        grad_k = jnp.einsum('rhk,rhd->kd', grad_score, query_heads) * score_scale
        grad_v = jnp.einsum('rhk,rhd->kd', rounded_weights, grad_heads)
        new_totals = (totals[0] + grad_k[:P_SIZE], totals[1] + grad_v[:P_SIZE])
        return new_totals, (grad_q.reshape(LMAX, HEADS * HEAD), grad_k[P_SIZE:], grad_v[P_SIZE:])

    zeros = jnp.zeros((P_SIZE, HEAD), jnp.float32)
    totals, outputs = lax.scan(per_response, (zeros, zeros), (queries, grad_out, keys_resp, values_resp, lengths))
    natural_grads, reply_keygrad, reply_valgrad = outputs
    blocks = natural_grads.reshape(NRESP, NBLK, RBLK, HEADS * HEAD)
    chosen = jnp.take_along_axis(blocks, block_plan.astype(jnp.int32)[:, :, None, None], axis=1)
    query_grads = chosen.reshape(NRESP, LMAX, HEADS * HEAD)
    return query_grads, totals[0], totals[1], reply_keygrad, reply_valgrad
```

```python
import functools
import math

import jax
import jax.numpy as jnp
from jax import lax
from jax.experimental import pallas as pl
from jax.experimental.pallas import tpu as pltpu
from jax.sharding import PartitionSpec as P

RBLK = 128
CHUNK = 256
MESH = pl.DeviceIdType.MESH
F32 = jnp.float32
BF16 = jnp.bfloat16


def remote(src, dst, send_sem, recv_sem, device):
    return pltpu.make_async_remote_copy(
        src_ref=src,
        dst_ref=dst,
        send_sem=send_sem,
        recv_sem=recv_sem,
        device_id=device,
        device_id_type=MESH,
    )


def dot_nt(a, b):
    return lax.dot_general(a, b, (((1,), (1,)), ((), ())), preferred_element_type=F32)


def dot_nn(a, b):
    return lax.dot_general(a, b, (((1,), (0,)), ((), ())), preferred_element_type=F32)


def kernel(
    chips, heads, per_step,
    len_ref, plan_ref, q_hbm, g_hbm, kr_hbm, vr_hbm, kp_hbm, vp_hbm,
    dq_hbm, pk_out, pv_out, rk_out, rv_out,
    raw, sb, wk, kv, kt, pt, dt, dq, tb, rb, s2, r2, rt, rr,
    local_sem, pair_send, pair_recv, gat_send, gat_recv, fwd_send, fwd_recv,
    sum_send, sum_recv, out_send, out_recv,
):
    me = lax.axis_index("prompt")
    core = lax.axis_index("resp")
    partner = {"resp": 1 - core}
    shard = kp_hbm.shape[0]
    half = shard // 2
    prefix_len = chips * shard
    own_keys = kr_hbm.shape[1]
    reply_len = 2 * own_keys
    scale = kv.shape[2] ** (-0.5)
    soft = scale * math.log2(math.e)

    barrier = pltpu.get_barrier_semaphore()
    for k in range(1, chips):
        pl.semaphore_signal(
            barrier, inc=1, device_id={"prompt": lax.rem(me + k, chips)}, device_id_type=MESH
        )
    pl.semaphore_signal(barrier, inc=1, device_id=partner, device_id_type=MESH)

    own_rows = pl.ds(pl.multiple_of(prefix_len + core * own_keys, own_keys), own_keys)
    chip_rows = pl.ds(pl.multiple_of(me * shard, shard), shard)
    loads = [
        pltpu.make_async_copy(kp_hbm, kv.at[0, chip_rows], local_sem.at[0]),
        pltpu.make_async_copy(vp_hbm, kv.at[1, chip_rows], local_sem.at[1]),
        pltpu.make_async_copy(kr_hbm.at[0], kv.at[0, own_rows], local_sem.at[2]),
        pltpu.make_async_copy(vr_hbm.at[0], kv.at[1, own_rows], local_sem.at[3]),
        pltpu.make_async_copy(q_hbm, raw.at[0], local_sem.at[4]),
        pltpu.make_async_copy(g_hbm, raw.at[1], local_sem.at[5]),
    ]
    for load in loads:
        load.start()

    length = len_ref[0]
    first, second = plan_ref[0, 0], plan_ref[0, 1]
    own_block = jnp.where(first // 2 == core, first, second)
    other_block = jnp.where(first // 2 == core, second, first)
    own_local = lax.rem(own_block, 2)
    sent_local = 1 - own_local
    sent_block = 2 * core + sent_local

    loads[0].wait()
    loads[1].wait()
    pl.semaphore_wait(barrier, chips)

    def half_rows(chip):
        return pl.ds(pl.multiple_of(chip * shard + core * half, half), half)

    mine = kv.at[:, half_rows(me)]
    gathers = []
    for k in range(1, chips):
        to = lax.rem(me + k, chips)
        copy = remote(mine, mine, gat_send.at[k], gat_recv.at[me], {"prompt": to})
        copy.start()
        gathers.append(copy)
    loads[2].wait()
    loads[3].wait()
    pair_kv = remote(
        kv.at[:, own_rows], kv.at[:, own_rows], pair_send.at[0], pair_recv.at[0], partner
    )
    pair_kv.start()
    loads[4].wait()
    loads[5].wait()

    def stack(block_local, block, target):
        rows = lax.broadcasted_iota(jnp.int32, (RBLK, 128), 0) + block * RBLK
        live = rows < length
        for h in range(heads):
            lanes = slice(h * 128, (h + 1) * 128)
            place = (h * RBLK) // CHUNK
            inner = slice((h * RBLK) % CHUNK, (h * RBLK) % CHUNK + RBLK)
            target[0, place, inner, :] = raw[0, block_local, :, lanes]
            grads = raw[1, block_local, :, lanes]
            target[1, place, inner, :] = jnp.where(live, grads, jnp.zeros_like(grads))

    stack(sent_local, sent_block, sb)
    pair_q = remote(sb, wk.at[1], pair_send.at[1], pair_recv.at[1], partner)
    pair_q.start()
    stack(own_local, own_block, wk.at[0])

    forwards = []
    for k in range(1, chips):
        source = lax.rem(me + chips - k, chips)
        there = kv.at[:, half_rows(source)]
        remote(there, there, gat_send.at[k], gat_recv.at[source], partner).wait_recv()
        copy = remote(there, there, fwd_send.at[k], fwd_recv.at[k], partner)
        copy.start()
        forwards.append(copy)
    for copy in forwards:
        copy.wait_recv()
    pair_kv.wait_recv()
    kt[...] = kv[0].astype(F32).T.astype(BF16)

    for step in range(2):
        block = own_block if step == 0 else other_block
        if step == 1:
            pair_q.wait_recv()

        def rows_chunk(j, carry):
            lane = lax.broadcasted_iota(jnp.int32, (1, CHUNK), 1)
            limit = jnp.minimum(block * RBLK + lax.rem(lane, RBLK), length - 1)
            scores = dot_nt(kv[0], wk[step, 0, j])
            spot = lax.broadcasted_iota(jnp.int32, (reply_len, CHUNK), 0)
            scores = jnp.concatenate(
                [
                    scores[:prefix_len],
                    jnp.where(spot <= limit, scores[prefix_len:], -jnp.inf),
                ],
                0,
            )
            top = jnp.max(scores, 0, keepdims=True)
            e = jnp.exp2((scores - top) * soft)
            inv = 1.0 / jnp.sum(e, 0, keepdims=True)
            gw = dot_nt(kv[1], wk[step, 1, j])
            weights = e * inv
            inner = jnp.sum(weights * gw, 0, keepdims=True)
            gs = (weights * (gw - inner)).astype(BF16)
            pt[step * per_step + j] = weights.astype(BF16)
            dt[step * per_step + j] = gs
            gq = dot_nn(kt[...], gs) * scale
            dq[step, j] = gq.T
            return carry

        lax.fori_loop(0, per_step, rows_chunk, 0)

    stores = []
    for step in range(2):
        for h in range(heads):
            place = (h * RBLK) // CHUNK
            inner = slice((h * RBLK) % CHUNK, (h * RBLK) % CHUNK + RBLK)
            copy = pltpu.make_async_copy(
                dq.at[step, place, inner, :],
                dq_hbm.at[step, :, pl.ds(h * 128, 128)],
                local_sem.at[6 + step * heads + h],
            )
            copy.start()
            stores.append(copy)

    def totals(start, size):
        rows = slice(start, start + size)
        k_sum = v_sum = None
        for i in range(2 * per_step):
            s, j = i // per_step, i % per_step
            k_part = dot_nn(dt[i, rows, :], wk[s, 0, j])
            v_part = dot_nn(pt[i, rows, :], wk[s, 1, j])
            k_sum = k_part if k_sum is None else k_sum + k_part
            v_sum = v_part if v_sum is None else v_sum + v_part
        return k_sum * scale, v_sum

    per = 256 // shard
    count = chips // per
    sums = []
    for n in range(count):
        k_sum, v_sum = totals(n * 256, 256)
        for which, value in ((0, k_sum), (1, v_sum)):
            value = value.reshape(per, 2, half, 128)
            for c in range(2):
                tb[c, n * per : (n + 1) * per, which] = value[:, c]
        span = pl.ds(n * per, per)
        copy = remote(tb.at[1 - core, span], rb.at[span], sum_send.at[n], sum_recv.at[n], partner)
        copy.start()
        sums.append(copy)

    outs = []

    def send_out(n):
        sums[n].wait_recv()
        span = slice(n * per, (n + 1) * per)
        s2[span] = (tb[core, span] + rb[span]).astype(BF16)
        for i in range(per):
            to = n * per + i

            @pl.when(to != me)
            def _():
                remote(
                    s2.at[to], r2.at[me], out_send.at[to], out_recv.at[me], {"prompt": to}
                ).start()

    for n in range(count - 1):
        send_out(n)
    k_sum, v_sum = totals(prefix_len, reply_len)
    for c in range(2):
        rt[c, 0] = k_sum[c * own_keys : (c + 1) * own_keys]
        rt[c, 1] = v_sum[c * own_keys : (c + 1) * own_keys]
    pair_r = remote(rt.at[1 - core], rr, pair_send.at[2], pair_recv.at[2], partner)
    pair_r.start()
    send_out(count - 1)

    pair_r.wait_recv()
    rk_out[0] = rt[core, 0] + rr[0]
    rv_out[0] = rt[core, 1] + rr[1]

    total = tb[core, me] + rb[me]
    for k in range(1, chips):
        source = lax.rem(me + chips - k, chips)
        remote(
            s2.at[source], r2.at[source], out_send.at[source], out_recv.at[source], partner
        ).wait_recv()
        total = total + r2[source].astype(F32)
    pk_out[...] = total[0]
    pv_out[...] = total[1]

    for k in range(1, chips):
        to = lax.rem(me + k, chips)
        remote(s2.at[to], r2.at[me], out_send.at[to], out_recv.at[me], {"prompt": to}).wait_send()
    for copy in gathers + forwards + sums + [pair_kv, pair_q, pair_r]:
        copy.wait_send()
    for copy in stores:
        copy.wait()


def solution(mesh):
    chips = mesh.shape["prompt"]

    def local(
        queries, grad_out, keys_resp, values_resp, keys_prefix, values_prefix, lengths, block_plan
    ):
        slots, width = queries.shape[1:]
        shard, head = keys_prefix.shape
        heads = width // head
        half = shard // 2
        blocks = slots // RBLK
        own_keys = keys_resp.shape[1]
        keys = chips * shard + 2 * own_keys
        per_step = heads * RBLK // CHUNK
        count = chips // (256 // shard)
        vm = pltpu.VMEM
        dma = pltpu.SemaphoreType.DMA
        any_spec = pl.BlockSpec(memory_space=pl.ANY)
        smem = pl.BlockSpec(memory_space=pltpu.SMEM)
        vmem = pl.BlockSpec(memory_space=pltpu.VMEM)
        dq, pk, pv, rk, rv = pl.pallas_call(
            functools.partial(kernel, chips, heads, per_step),
            out_shape=(
                jax.ShapeDtypeStruct((blocks, RBLK, width), F32),
                jax.ShapeDtypeStruct((half, head), F32),
                jax.ShapeDtypeStruct((half, head), F32),
                jax.ShapeDtypeStruct((1, own_keys, head), F32),
                jax.ShapeDtypeStruct((1, own_keys, head), F32),
            ),
            in_specs=[smem, smem] + [any_spec] * 6,
            out_specs=(any_spec, vmem, vmem, vmem, vmem),
            scratch_shapes=[
                vm((2, blocks, RBLK, width), BF16),
                vm((2, per_step, CHUNK, head), BF16),
                vm((2, 2, per_step, CHUNK, head), BF16),
                vm((2, keys, head), BF16),
                vm((head, keys), BF16),
                vm((2 * per_step, keys, CHUNK), BF16),
                vm((2 * per_step, keys, CHUNK), BF16),
                vm((2, per_step, CHUNK, head), F32),
                vm((2, chips, 2, half, head), F32),
                vm((chips, 2, half, head), F32),
                vm((chips, 2, half, head), BF16),
                vm((chips, 2, half, head), BF16),
                vm((2, 2, own_keys, head), F32),
                vm((2, own_keys, head), F32),
                dma((6 + 2 * heads,)),
                dma((3,)),
                dma((3,)),
                dma((chips,)),
                dma((chips,)),
                dma((chips,)),
                dma((chips,)),
                dma((count,)),
                dma((count,)),
                dma((chips,)),
                dma((chips,)),
            ],
            compiler_params=pltpu.CompilerParams(
                collective_id=0, has_side_effects=True, vmem_limit_bytes=60 * 1024 * 1024
            ),
        )(
            lengths,
            block_plan,
            queries.reshape(blocks, RBLK, width),
            grad_out.reshape(blocks, RBLK, width),
            keys_resp,
            values_resp,
            keys_prefix,
            values_prefix,
        )
        in_order = block_plan[0, 0] // blocks == lax.axis_index("resp")
        dq = jnp.where(in_order, dq, dq[::-1])
        return dq.reshape(1, slots, width), pk, pv, rk, rv

    placed = (
        P(("groups", "prompt"), "resp", None),
        P(("groups", "prompt"), "resp", None),
        P(("groups", "prompt"), "resp", None),
        P(("groups", "prompt"), "resp", None),
        P(("groups", "prompt"), None),
        P(("groups", "prompt"), None),
        P(("groups", "prompt")),
        P(("groups", "prompt"), "resp"),
    )
    return jax.shard_map(
        local,
        mesh=mesh,
        in_specs=placed,
        out_specs=(
            P(("groups", "prompt"), "resp", None),
            P(("groups", "prompt", "resp"), None),
            P(("groups", "prompt", "resp"), None),
            P(("groups", "prompt"), "resp", None),
            P(("groups", "prompt"), "resp", None),
        ),
        check_vma=False,
    )
```

```python
import functools
import math

import jax
import jax.numpy as jnp
from jax import lax
from jax.experimental import pallas as pl
from jax.experimental.pallas import tpu as pltpu
from jax.sharding import PartitionSpec as P

RBLK = 128
CHUNK = 256
MESH = pl.DeviceIdType.MESH
F32 = jnp.float32
BF16 = jnp.bfloat16


def remote(src, dst, send_sem, recv_sem, device):
    return pltpu.make_async_remote_copy(
        src_ref=src,
        dst_ref=dst,
        send_sem=send_sem,
        recv_sem=recv_sem,
        device_id=device,
        device_id_type=MESH,
    )


def dot_nt(a, b):
    return lax.dot_general(a, b, (((1,), (1,)), ((), ())), preferred_element_type=F32)


def dot_nn(a, b):
    return lax.dot_general(a, b, (((1,), (0,)), ((), ())), preferred_element_type=F32)


def kernel(
    chips, heads, per_step,
    len_ref, plan_ref, q_hbm, g_hbm, kr_hbm, vr_hbm, kp_hbm, vp_hbm,
    dq, pk_out, pv_out, rk_out, rv_out,
    raw, sb, wk, kv, kt, pt, dt, tb, rb, s2, r2, rt, rr,
    local_sem, pair_send, pair_recv, gat_send, gat_recv, fwd_send, fwd_recv,
    sum_send, sum_recv, out_send, out_recv,
):
    me = lax.axis_index("prompt")
    core = lax.axis_index("resp")
    partner = {"resp": 1 - core}
    shard = kp_hbm.shape[0]
    half = shard // 2
    prefix_len = chips * shard
    own_keys = kr_hbm.shape[1]
    reply_len = 2 * own_keys
    scale = kv.shape[2] ** (-0.5)
    soft = scale * math.log2(math.e)

    barrier = pltpu.get_barrier_semaphore()
    for k in range(1, chips):
        pl.semaphore_signal(
            barrier, inc=1, device_id={"prompt": lax.rem(me + k, chips)}, device_id_type=MESH
        )
    pl.semaphore_signal(barrier, inc=1, device_id=partner, device_id_type=MESH)

    own_rows = pl.ds(pl.multiple_of(prefix_len + core * own_keys, own_keys), own_keys)
    chip_rows = pl.ds(pl.multiple_of(me * shard, shard), shard)
    loads = [
        pltpu.make_async_copy(kp_hbm, kv.at[0, chip_rows], local_sem.at[0]),
        pltpu.make_async_copy(vp_hbm, kv.at[1, chip_rows], local_sem.at[1]),
        pltpu.make_async_copy(kr_hbm.at[0], kv.at[0, own_rows], local_sem.at[2]),
        pltpu.make_async_copy(vr_hbm.at[0], kv.at[1, own_rows], local_sem.at[3]),
        pltpu.make_async_copy(q_hbm, raw.at[0], local_sem.at[4]),
        pltpu.make_async_copy(g_hbm, raw.at[1], local_sem.at[5]),
    ]
    for load in loads:
        load.start()

    length = len_ref[0]
    first, second = plan_ref[0, 0], plan_ref[0, 1]
    own_block = jnp.where(first // 2 == core, first, second)
    other_block = jnp.where(first // 2 == core, second, first)
    own_local = lax.rem(own_block, 2)
    sent_local = 1 - own_local
    sent_block = 2 * core + sent_local

    loads[0].wait()
    loads[1].wait()
    pl.semaphore_wait(barrier, chips)

    def half_rows(chip):
        return pl.ds(pl.multiple_of(chip * shard + core * half, half), half)

    mine = kv.at[:, half_rows(me)]
    gathers = []
    for k in range(1, chips):
        to = lax.rem(me + k, chips)
        copy = remote(mine, mine, gat_send.at[k], gat_recv.at[me], {"prompt": to})
        copy.start()
        gathers.append(copy)
    loads[2].wait()
    loads[3].wait()
    pair_kv = remote(
        kv.at[:, own_rows], kv.at[:, own_rows], pair_send.at[0], pair_recv.at[0], partner
    )
    pair_kv.start()
    loads[4].wait()
    loads[5].wait()

    def stack(block_local, block, target):
        rows = lax.broadcasted_iota(jnp.int32, (RBLK, 128), 0) + block * RBLK
        live = rows < length
        for h in range(heads):
            lanes = slice(h * 128, (h + 1) * 128)
            place = (h * RBLK) // CHUNK
            inner = slice((h * RBLK) % CHUNK, (h * RBLK) % CHUNK + RBLK)
            target[0, place, inner, :] = raw[0, block_local, :, lanes]
            grads = raw[1, block_local, :, lanes]
            target[1, place, inner, :] = jnp.where(live, grads, jnp.zeros_like(grads))

    stack(sent_local, sent_block, sb)
    pair_q = remote(sb, wk.at[1], pair_send.at[1], pair_recv.at[1], partner)
    pair_q.start()
    stack(own_local, own_block, wk.at[0])

    forwards = []
    for k in range(1, chips):
        source = lax.rem(me + chips - k, chips)
        there = kv.at[:, half_rows(source)]
        remote(there, there, gat_send.at[k], gat_recv.at[source], partner).wait_recv()
        copy = remote(there, there, fwd_send.at[k], fwd_recv.at[k], partner)
        copy.start()
        forwards.append(copy)
    for copy in forwards:
        copy.wait_recv()
    pair_kv.wait_recv()
    kt[...] = kv[0].astype(F32).T.astype(BF16)

    for step in range(2):
        block = own_block if step == 0 else other_block
        if step == 1:
            pair_q.wait_recv()

        def rows_chunk(j, carry):
            lane = lax.broadcasted_iota(jnp.int32, (1, CHUNK), 1)
            limit = jnp.minimum(block * RBLK + lax.rem(lane, RBLK), length - 1)
            scores = dot_nt(kv[0], wk[step, 0, j])
            spot = lax.broadcasted_iota(jnp.int32, (reply_len, CHUNK), 0)
            scores = jnp.concatenate(
                [
                    scores[:prefix_len],
                    jnp.where(spot <= limit, scores[prefix_len:], -jnp.inf),
                ],
                0,
            )
            top = jnp.max(scores, 0, keepdims=True)
            e = jnp.exp2((scores - top) * soft)
            inv = 1.0 / jnp.sum(e, 0, keepdims=True)
            gw = dot_nt(kv[1], wk[step, 1, j])
            weights = e * inv
            inner = jnp.sum(weights * gw, 0, keepdims=True)
            gs = (weights * (gw - inner)).astype(BF16)
            pt[step * per_step + j] = weights.astype(BF16)
            dt[step * per_step + j] = gs
            gq = dot_nn(kt[...], gs) * scale
            gq = gq.T
            for i in range(CHUNK // RBLK):
                lanes = pl.multiple_of((j * (CHUNK // RBLK) + i) * 128, 128)
                dq[step, :, pl.ds(lanes, 128)] = gq[i * RBLK : (i + 1) * RBLK]
            return carry

        lax.fori_loop(0, per_step, rows_chunk, 0)

    def totals(start, size):
        rows = slice(start, start + size)
        k_sum = v_sum = None
        for i in range(2 * per_step):
            s, j = i // per_step, i % per_step
            k_part = dot_nn(dt[i, rows, :], wk[s, 0, j])
            v_part = dot_nn(pt[i, rows, :], wk[s, 1, j])
            k_sum = k_part if k_sum is None else k_sum + k_part
            v_sum = v_part if v_sum is None else v_sum + v_part
        return k_sum * scale, v_sum

    per = 256 // shard
    count = chips // per
    sums = []
    for n in range(count):
        k_sum, v_sum = totals(n * 256, 256)
        for which, value in ((0, k_sum), (1, v_sum)):
            value = value.reshape(per, 2, half, 128)
            for c in range(2):
                tb[c, n * per : (n + 1) * per, which] = value[:, c]
        span = pl.ds(n * per, per)
        copy = remote(tb.at[1 - core, span], rb.at[span], sum_send.at[n], sum_recv.at[n], partner)
        copy.start()
        sums.append(copy)

    outs = []

    def send_out(n):
        sums[n].wait_recv()
        span = slice(n * per, (n + 1) * per)
        s2[span] = (tb[core, span] + rb[span]).astype(BF16)
        for i in range(per):
            to = n * per + i

            @pl.when(to != me)
            def _():
                remote(
                    s2.at[to], r2.at[me], out_send.at[to], out_recv.at[me], {"prompt": to}
                ).start()

    for n in range(count - 1):
        send_out(n)
    k_sum, v_sum = totals(prefix_len, reply_len)
    for c in range(2):
        rt[c, 0] = k_sum[c * own_keys : (c + 1) * own_keys]
        rt[c, 1] = v_sum[c * own_keys : (c + 1) * own_keys]
    pair_r = remote(rt.at[1 - core], rr, pair_send.at[2], pair_recv.at[2], partner)
    pair_r.start()
    send_out(count - 1)

    pair_r.wait_recv()
    rk_out[0] = rt[core, 0] + rr[0]
    rv_out[0] = rt[core, 1] + rr[1]

    total = tb[core, me] + rb[me]
    for k in range(1, chips):
        source = lax.rem(me + chips - k, chips)
        remote(
            s2.at[source], r2.at[source], out_send.at[source], out_recv.at[source], partner
        ).wait_recv()
        total = total + r2[source].astype(F32)
    pk_out[...] = total[0]
    pv_out[...] = total[1]

    for k in range(1, chips):
        to = lax.rem(me + k, chips)
        remote(s2.at[to], r2.at[me], out_send.at[to], out_recv.at[me], {"prompt": to}).wait_send()
    for copy in gathers + forwards + sums + [pair_kv, pair_q, pair_r]:
        copy.wait_send()


def finish(plan_ref, dq, pk, pv, rk, rv, dq_out, pk_out, pv_out, rk_out, rv_out, sem):
    core = lax.axis_index("resp")
    copies = []
    for s in range(dq.shape[0]):
        step = jnp.where(plan_ref[0, s] // 2 == core, 0, 1)
        rows = pl.ds(s * RBLK, RBLK)
        copies.append(pltpu.make_async_copy(dq.at[step], dq_out.at[0, rows], sem.at[s]))
    for i, (src, dst) in enumerate(((pk, pk_out), (pv, pv_out), (rk, rk_out), (rv, rv_out))):
        copies.append(pltpu.make_async_copy(src, dst, sem.at[dq.shape[0] + i]))
    for copy in copies:
        copy.start()
    for copy in copies:
        copy.wait()


def solution(mesh):
    chips = mesh.shape["prompt"]

    def local(
        queries, grad_out, keys_resp, values_resp, keys_prefix, values_prefix, lengths, block_plan
    ):
        slots, width = queries.shape[1:]
        shard, head = keys_prefix.shape
        heads = width // head
        half = shard // 2
        blocks = slots // RBLK
        own_keys = keys_resp.shape[1]
        keys = chips * shard + 2 * own_keys
        per_step = heads * RBLK // CHUNK
        count = chips // (256 // shard)
        vm = pltpu.VMEM
        dma = pltpu.SemaphoreType.DMA
        any_spec = pl.BlockSpec(memory_space=pl.ANY)
        smem = pl.BlockSpec(memory_space=pltpu.SMEM)
        vmem = pl.BlockSpec(memory_space=pltpu.VMEM)
        shapes = (
            (blocks, RBLK, width),
            (half, head),
            (half, head),
            (1, own_keys, head),
            (1, own_keys, head),
        )
        parts = pl.pallas_call(
            functools.partial(kernel, chips, heads, per_step),
            out_shape=tuple(vm(shape, F32) for shape in shapes),
            in_specs=[smem, smem] + [any_spec] * 6,
            out_specs=(vmem,) * 5,
            scratch_shapes=[
                vm((2, blocks, RBLK, width), BF16),
                vm((2, per_step, CHUNK, head), BF16),
                vm((2, 2, per_step, CHUNK, head), BF16),
                vm((2, keys, head), BF16),
                vm((head, keys), BF16),
                vm((2 * per_step, keys, CHUNK), BF16),
                vm((2 * per_step, keys, CHUNK), BF16),
                vm((2, chips, 2, half, head), F32),
                vm((chips, 2, half, head), F32),
                vm((chips, 2, half, head), BF16),
                vm((chips, 2, half, head), BF16),
                vm((2, 2, own_keys, head), F32),
                vm((2, own_keys, head), F32),
                dma((6,)),
                dma((3,)),
                dma((3,)),
                dma((chips,)),
                dma((chips,)),
                dma((chips,)),
                dma((chips,)),
                dma((count,)),
                dma((count,)),
                dma((chips,)),
                dma((chips,)),
            ],
            compiler_params=pltpu.CompilerParams(
                collective_id=0, has_side_effects=True, vmem_limit_bytes=60 * 1024 * 1024
            ),
        )(
            lengths,
            block_plan,
            queries.reshape(blocks, RBLK, width),
            grad_out.reshape(blocks, RBLK, width),
            keys_resp,
            values_resp,
            keys_prefix,
            values_prefix,
        )
        parts = [pltpu.with_memory_space_constraint(part, pltpu.VMEM) for part in parts]
        shapes = ((1, slots, width),) + shapes[1:]
        return pl.pallas_call(
            finish,
            out_shape=tuple(jax.ShapeDtypeStruct(shape, F32) for shape in shapes),
            in_specs=[smem] + [vmem] * 5,
            out_specs=(any_spec,) * 5,
            scratch_shapes=[dma((blocks + 4,))],
        )(block_plan, *parts)

    placed = (
        P(("groups", "prompt"), "resp", None),
        P(("groups", "prompt"), "resp", None),
        P(("groups", "prompt"), "resp", None),
        P(("groups", "prompt"), "resp", None),
        P(("groups", "prompt"), None),
        P(("groups", "prompt"), None),
        P(("groups", "prompt")),
        P(("groups", "prompt"), "resp"),
    )
    return jax.shard_map(
        local,
        mesh=mesh,
        in_specs=placed,
        out_specs=(
            P(("groups", "prompt"), "resp", None),
            P(("groups", "prompt", "resp"), None),
            P(("groups", "prompt", "resp"), None),
            P(("groups", "prompt"), "resp", None),
            P(("groups", "prompt"), "resp", None),
        ),
        check_vma=False,
    )
```

```python
import functools
import math

import jax
import jax.numpy as jnp
from jax import lax
from jax.experimental import pallas as pl
from jax.experimental.pallas import tpu as pltpu
from jax.sharding import PartitionSpec as P

RBLK = 128
CHUNK = 256
MESH = pl.DeviceIdType.MESH
F32 = jnp.float32
BF16 = jnp.bfloat16


def remote(src, dst, send_sem, recv_sem, device):
    return pltpu.make_async_remote_copy(
        src_ref=src,
        dst_ref=dst,
        send_sem=send_sem,
        recv_sem=recv_sem,
        device_id=device,
        device_id_type=MESH,
    )


def dot_nt(a, b):
    return lax.dot_general(a, b, (((1,), (1,)), ((), ())), preferred_element_type=F32)


def dot_nn(a, b):
    return lax.dot_general(a, b, (((1,), (0,)), ((), ())), preferred_element_type=F32)


def kernel(
    chips, heads, per_step,
    len_ref, plan_ref, q_hbm, g_hbm, kr_hbm, vr_hbm, kp_hbm, vp_hbm,
    dq, pk_out, pv_out, rk_out, rv_out,
    raw, sb, wk, kv, kt, pt, dt, tb, rb, s2, r2, rt, rr,
    local_sem, pair_send, pair_recv, gat_send, gat_recv, fwd_send, fwd_recv,
    sum_send, sum_recv, out_send, out_recv,
):
    me = lax.axis_index("prompt")
    core = lax.axis_index("resp")
    partner = {"resp": 1 - core}
    shard = kp_hbm.shape[0]
    half = shard // 2
    prefix_len = chips * shard
    own_keys = kr_hbm.shape[1]
    reply_len = 2 * own_keys
    scale = kv.shape[2] ** (-0.5)
    soft = scale * math.log2(math.e)

    barrier = pltpu.get_barrier_semaphore()
    for k in range(1, chips):
        pl.semaphore_signal(
            barrier, inc=1, device_id={"prompt": lax.rem(me + k, chips)}, device_id_type=MESH
        )
    pl.semaphore_signal(barrier, inc=1, device_id=partner, device_id_type=MESH)

    own_rows = pl.ds(pl.multiple_of(prefix_len + core * own_keys, own_keys), own_keys)
    chip_rows = pl.ds(pl.multiple_of(me * shard, shard), shard)
    loads = [
        pltpu.make_async_copy(kp_hbm, kv.at[0, chip_rows], local_sem.at[0]),
        pltpu.make_async_copy(vp_hbm, kv.at[1, chip_rows], local_sem.at[1]),
        pltpu.make_async_copy(kr_hbm.at[0], kv.at[0, own_rows], local_sem.at[2]),
        pltpu.make_async_copy(vr_hbm.at[0], kv.at[1, own_rows], local_sem.at[3]),
        pltpu.make_async_copy(q_hbm, raw.at[0], local_sem.at[4]),
        pltpu.make_async_copy(g_hbm, raw.at[1], local_sem.at[5]),
    ]
    for load in loads:
        load.start()

    length = len_ref[0]
    first, second = plan_ref[0, 0], plan_ref[0, 1]
    own_block = jnp.where(first // 2 == core, first, second)
    other_block = jnp.where(first // 2 == core, second, first)
    own_local = lax.rem(own_block, 2)
    sent_local = 1 - own_local
    sent_block = 2 * core + sent_local

    loads[0].wait()
    loads[1].wait()
    pl.semaphore_wait(barrier, chips)

    def half_rows(chip):
        return pl.ds(pl.multiple_of(chip * shard + core * half, half), half)

    mine = kv.at[:, half_rows(me)]
    gathers = []
    for k in range(1, chips):
        to = lax.rem(me + k, chips)
        copy = remote(mine, mine, gat_send.at[k], gat_recv.at[me], {"prompt": to})
        copy.start()
        gathers.append(copy)
    loads[2].wait()
    loads[3].wait()
    pair_kv = remote(
        kv.at[:, own_rows], kv.at[:, own_rows], pair_send.at[0], pair_recv.at[0], partner
    )
    pair_kv.start()
    loads[4].wait()
    loads[5].wait()

    def stack(block_local, block, target):
        rows = lax.broadcasted_iota(jnp.int32, (RBLK, 128), 0) + block * RBLK
        live = rows < length
        for h in range(heads):
            lanes = slice(h * 128, (h + 1) * 128)
            place = (h * RBLK) // CHUNK
            inner = slice((h * RBLK) % CHUNK, (h * RBLK) % CHUNK + RBLK)
            target[0, place, inner, :] = raw[0, block_local, :, lanes]
            grads = raw[1, block_local, :, lanes]
            target[1, place, inner, :] = jnp.where(live, grads, jnp.zeros_like(grads))

    stack(sent_local, sent_block, sb)
    pair_q = remote(sb, wk.at[1], pair_send.at[1], pair_recv.at[1], partner)
    pair_q.start()
    stack(own_local, own_block, wk.at[0])

    forwards = []
    for k in range(1, chips):
        source = lax.rem(me + chips - k, chips)
        there = kv.at[:, half_rows(source)]
        remote(there, there, gat_send.at[k], gat_recv.at[source], partner).wait_recv()
        copy = remote(there, there, fwd_send.at[k], fwd_recv.at[k], partner)
        copy.start()
        forwards.append(copy)
    for copy in forwards:
        copy.wait_recv()
    pair_kv.wait_recv()

    pair_q.wait_recv()
    keys_of = (prefix_len + own_keys, prefix_len + reply_len)
    low_block = jnp.where(core == 0, own_block, other_block)
    high_block = jnp.where(core == 0, other_block, own_block)
    place_of = (core, 1 - core)

    for level, block in ((0, low_block), (1, high_block)):
        keys = keys_of[level]
        place = place_of[level]

        def rows_chunk(j, carry):
            lane = lax.broadcasted_iota(jnp.int32, (1, CHUNK), 1)
            limit = jnp.minimum(block * RBLK + lax.rem(lane, RBLK), length - 1)
            scores = dot_nt(kv[0, :keys], wk[place, 0, j])
            spot = lax.broadcasted_iota(jnp.int32, (keys - prefix_len, CHUNK), 0)
            scores = jnp.concatenate(
                [
                    scores[:prefix_len],
                    jnp.where(spot <= limit, scores[prefix_len:], -jnp.inf),
                ],
                0,
            )
            top = jnp.max(scores, 0, keepdims=True)
            e = jnp.exp2((scores - top) * soft)
            inv = 1.0 / jnp.sum(e, 0, keepdims=True)
            gw = dot_nt(kv[1, :keys], wk[place, 1, j])
            weights = e * inv
            inner = jnp.sum(weights * gw, 0, keepdims=True)
            pt[level * per_step + j, :keys] = weights.astype(BF16)
            dt[level * per_step + j, :keys] = (weights * (gw - inner)).astype(BF16)
            return carry

        lax.fori_loop(0, per_step, rows_chunk, 0)

    def totals(start, size, levels):
        rows = slice(start, start + size)
        k_sum = v_sum = None
        for level in levels:
            for j in range(per_step):
                i = level * per_step + j
                k_part = dot_nn(dt[i, rows, :], wk[place_of[level], 0, j])
                v_part = dot_nn(pt[i, rows, :], wk[place_of[level], 1, j])
                k_sum = k_part if k_sum is None else k_sum + k_part
                v_sum = v_part if v_sum is None else v_sum + v_part
        return k_sum * scale, v_sum

    per = 256 // shard
    count = chips // per
    sums = []
    for n in range(count):
        k_sum, v_sum = totals(n * 256, 256, (0, 1))
        for which, value in ((0, k_sum), (1, v_sum)):
            value = value.reshape(per, 2, half, 128)
            for c in range(2):
                tb[c, n * per : (n + 1) * per, which] = value[:, c]
        span = pl.ds(n * per, per)
        copy = remote(tb.at[1 - core, span], rb.at[span], sum_send.at[n], sum_recv.at[n], partner)
        copy.start()
        sums.append(copy)

    outs = []

    def send_out(n):
        sums[n].wait_recv()
        span = slice(n * per, (n + 1) * per)
        s2[span] = (tb[core, span] + rb[span]).astype(BF16)
        for i in range(per):
            to = n * per + i

            @pl.when(to != me)
            def _():
                remote(
                    s2.at[to], r2.at[me], out_send.at[to], out_recv.at[me], {"prompt": to}
                ).start()

    for c in range(2):
        k_sum, v_sum = totals(prefix_len + c * own_keys, own_keys, (0, 1) if c == 0 else (1,))
        rt[c, 0] = k_sum
        rt[c, 1] = v_sum
        if c < count - 1:
            send_out(c)
    pair_r = remote(rt.at[1 - core], rr, pair_send.at[2], pair_recv.at[2], partner)
    pair_r.start()
    for n in range(min(2, count - 1), count):
        send_out(n)

    kt[...] = kv[0].astype(F32).T.astype(BF16)
    for level in range(2):
        keys = keys_of[level]
        place = place_of[level]

        def grads_chunk(j, carry):
            gq = (dot_nn(kt[:, :keys], dt[level * per_step + j, :keys]) * scale).T
            for i in range(CHUNK // RBLK):
                lanes = pl.multiple_of((j * (CHUNK // RBLK) + i) * 128, 128)
                dq[place, :, pl.ds(lanes, 128)] = gq[i * RBLK : (i + 1) * RBLK]
            return carry

        lax.fori_loop(0, per_step, grads_chunk, 0)

    pair_r.wait_recv()
    rk_out[0] = rt[core, 0] + rr[0]
    rv_out[0] = rt[core, 1] + rr[1]

    total = tb[core, me] + rb[me]
    for k in range(1, chips):
        source = lax.rem(me + chips - k, chips)
        remote(
            s2.at[source], r2.at[source], out_send.at[source], out_recv.at[source], partner
        ).wait_recv()
        total = total + r2[source].astype(F32)
    pk_out[...] = total[0]
    pv_out[...] = total[1]

    for k in range(1, chips):
        to = lax.rem(me + k, chips)
        remote(s2.at[to], r2.at[me], out_send.at[to], out_recv.at[me], {"prompt": to}).wait_send()
    for copy in gathers + forwards + sums + [pair_kv, pair_q, pair_r]:
        copy.wait_send()


def finish(plan_ref, dq, pk, pv, rk, rv, dq_out, pk_out, pv_out, rk_out, rv_out, sem):
    core = lax.axis_index("resp")
    copies = []
    for s in range(dq.shape[0]):
        step = jnp.where(plan_ref[0, s] // 2 == core, 0, 1)
        rows = pl.ds(s * RBLK, RBLK)
        copies.append(pltpu.make_async_copy(dq.at[step], dq_out.at[0, rows], sem.at[s]))
    for i, (src, dst) in enumerate(((pk, pk_out), (pv, pv_out), (rk, rk_out), (rv, rv_out))):
        copies.append(pltpu.make_async_copy(src, dst, sem.at[dq.shape[0] + i]))
    for copy in copies:
        copy.start()
    for copy in copies:
        copy.wait()


def solution(mesh):
    chips = mesh.shape["prompt"]

    def local(
        queries, grad_out, keys_resp, values_resp, keys_prefix, values_prefix, lengths, block_plan
    ):
        slots, width = queries.shape[1:]
        shard, head = keys_prefix.shape
        heads = width // head
        half = shard // 2
        blocks = slots // RBLK
        own_keys = keys_resp.shape[1]
        keys = chips * shard + 2 * own_keys
        per_step = heads * RBLK // CHUNK
        count = chips // (256 // shard)
        vm = pltpu.VMEM
        dma = pltpu.SemaphoreType.DMA
        any_spec = pl.BlockSpec(memory_space=pl.ANY)
        smem = pl.BlockSpec(memory_space=pltpu.SMEM)
        vmem = pl.BlockSpec(memory_space=pltpu.VMEM)
        shapes = (
            (blocks, RBLK, width),
            (half, head),
            (half, head),
            (1, own_keys, head),
            (1, own_keys, head),
        )
        parts = pl.pallas_call(
            functools.partial(kernel, chips, heads, per_step),
            out_shape=tuple(vm(shape, F32) for shape in shapes),
            in_specs=[smem, smem] + [any_spec] * 6,
            out_specs=(vmem,) * 5,
            scratch_shapes=[
                vm((2, blocks, RBLK, width), BF16),
                vm((2, per_step, CHUNK, head), BF16),
                vm((2, 2, per_step, CHUNK, head), BF16),
                vm((2, keys, head), BF16),
                vm((head, keys), BF16),
                vm((2 * per_step, keys, CHUNK), BF16),
                vm((2 * per_step, keys, CHUNK), BF16),
                vm((2, chips, 2, half, head), F32),
                vm((chips, 2, half, head), F32),
                vm((chips, 2, half, head), BF16),
                vm((chips, 2, half, head), BF16),
                vm((2, 2, own_keys, head), F32),
                vm((2, own_keys, head), F32),
                dma((6,)),
                dma((3,)),
                dma((3,)),
                dma((chips,)),
                dma((chips,)),
                dma((chips,)),
                dma((chips,)),
                dma((count,)),
                dma((count,)),
                dma((chips,)),
                dma((chips,)),
            ],
            compiler_params=pltpu.CompilerParams(
                collective_id=0, has_side_effects=True, vmem_limit_bytes=60 * 1024 * 1024
            ),
        )(
            lengths,
            block_plan,
            queries.reshape(blocks, RBLK, width),
            grad_out.reshape(blocks, RBLK, width),
            keys_resp,
            values_resp,
            keys_prefix,
            values_prefix,
        )
        parts = [pltpu.with_memory_space_constraint(part, pltpu.VMEM) for part in parts]
        shapes = ((1, slots, width),) + shapes[1:]
        return pl.pallas_call(
            finish,
            out_shape=tuple(jax.ShapeDtypeStruct(shape, F32) for shape in shapes),
            in_specs=[smem] + [vmem] * 5,
            out_specs=(any_spec,) * 5,
            scratch_shapes=[dma((blocks + 4,))],
        )(block_plan, *parts)

    placed = (
        P(("groups", "prompt"), "resp", None),
        P(("groups", "prompt"), "resp", None),
        P(("groups", "prompt"), "resp", None),
        P(("groups", "prompt"), "resp", None),
        P(("groups", "prompt"), None),
        P(("groups", "prompt"), None),
        P(("groups", "prompt")),
        P(("groups", "prompt"), "resp"),
    )
    return jax.shard_map(
        local,
        mesh=mesh,
        in_specs=placed,
        out_specs=(
            P(("groups", "prompt"), "resp", None),
            P(("groups", "prompt", "resp"), None),
            P(("groups", "prompt", "resp"), None),
            P(("groups", "prompt"), "resp", None),
            P(("groups", "prompt"), "resp", None),
        ),
        check_vma=False,
    )
```

```python
import functools
import math

import jax
import jax.numpy as jnp
from jax import lax
from jax.experimental import pallas as pl
from jax.experimental.pallas import tpu as pltpu
from jax.sharding import PartitionSpec as P

RBLK = 128
CHUNK = 256
HIDDEN = -1e30
MESH = pl.DeviceIdType.MESH
F32 = jnp.float32
BF16 = jnp.bfloat16


def remote(src, dst, send_sem, recv_sem, device):
    return pltpu.make_async_remote_copy(
        src_ref=src,
        dst_ref=dst,
        send_sem=send_sem,
        recv_sem=recv_sem,
        device_id=device,
        device_id_type=MESH,
    )


def dot_nt(a, b):
    return lax.dot_general(a, b, (((1,), (1,)), ((), ())), preferred_element_type=F32)


def dot_nn(a, b):
    return lax.dot_general(a, b, (((1,), (0,)), ((), ())), preferred_element_type=F32)


def kernel(
    chips, heads, per_step,
    len_ref, plan_ref, q_hbm, g_hbm, kr_hbm, vr_hbm, kp_hbm, vp_hbm,
    dq, pk_out, pv_out, rk_out, rv_out,
    raw, sb, wk, kv, kt, pt, dt, pr, dr, er, gr, stat, tb, rb, s2, r2, rt, rr,
    local_sem, pair_send, pair_recv, gat_send, gat_recv, fwd_send, fwd_recv,
    sum_send, sum_recv, out_send, out_recv,
):
    me = lax.axis_index("prompt")
    core = lax.axis_index("resp")
    partner = {"resp": 1 - core}
    shard = kp_hbm.shape[0]
    half = shard // 2
    prefix_len = chips * shard
    own_keys = kr_hbm.shape[1]
    reply_len = 2 * own_keys
    scale = kv.shape[2] ** (-0.5)
    soft = scale * math.log2(math.e)

    barrier = pltpu.get_barrier_semaphore()
    for k in range(1, chips):
        pl.semaphore_signal(
            barrier, inc=1, device_id={"prompt": lax.rem(me + k, chips)}, device_id_type=MESH
        )
    pl.semaphore_signal(barrier, inc=1, device_id=partner, device_id_type=MESH)

    own_rows = pl.ds(pl.multiple_of(prefix_len + core * own_keys, own_keys), own_keys)
    chip_rows = pl.ds(pl.multiple_of(me * shard, shard), shard)
    loads = [
        pltpu.make_async_copy(kp_hbm, kv.at[0, chip_rows], local_sem.at[0]),
        pltpu.make_async_copy(vp_hbm, kv.at[1, chip_rows], local_sem.at[1]),
        pltpu.make_async_copy(kr_hbm.at[0], kv.at[0, own_rows], local_sem.at[2]),
        pltpu.make_async_copy(vr_hbm.at[0], kv.at[1, own_rows], local_sem.at[3]),
        pltpu.make_async_copy(q_hbm, raw.at[0], local_sem.at[4]),
        pltpu.make_async_copy(g_hbm, raw.at[1], local_sem.at[5]),
    ]
    for load in loads:
        load.start()

    length = len_ref[0]
    first, second = plan_ref[0, 0], plan_ref[0, 1]
    own_block = jnp.where(first // 2 == core, first, second)
    other_block = jnp.where(first // 2 == core, second, first)
    own_local = lax.rem(own_block, 2)
    sent_local = 1 - own_local
    sent_block = 2 * core + sent_local

    for load in loads[2:]:
        load.wait()
    def stack(block_local, block, target):
        rows = lax.broadcasted_iota(jnp.int32, (RBLK, 128), 0) + block * RBLK
        live = rows < length
        for h in range(heads):
            lanes = slice(h * 128, (h + 1) * 128)
            place = (h * RBLK) // CHUNK
            inner = slice((h * RBLK) % CHUNK, (h * RBLK) % CHUNK + RBLK)
            target[0, place, inner, :] = raw[0, block_local, :, lanes]
            grads = raw[1, block_local, :, lanes]
            target[1, place, inner, :] = jnp.where(live, grads, jnp.zeros_like(grads))

    blocks_of = (jnp.where(core == 0, own_block, other_block), jnp.where(core == 0, other_block, own_block))
    place_of = (core, 1 - core)

    def piece(place, block, part, slot):
        keys = pl.ds(pl.multiple_of(prefix_len + part * own_keys, own_keys), own_keys)

        def rows_chunk(j, carry):
            lane = lax.broadcasted_iota(jnp.int32, (1, CHUNK), 1)
            limit = jnp.minimum(block * RBLK + lax.rem(lane, RBLK), length - 1)
            spot = lax.broadcasted_iota(jnp.int32, (own_keys, CHUNK), 0) + part * own_keys
            scores = dot_nt(kv[0, keys], wk[place, 0, j])
            scores = jnp.where(spot <= limit, scores, HIDDEN)
            top = jnp.max(scores, 0, keepdims=True)
            e = jnp.exp2((scores - top) * soft)
            gw = dot_nt(kv[1, keys], wk[place, 1, j])
            i = slot * per_step + j
            er[i] = e
            gr[i] = gw
            stat[0, i] = top
            stat[1, i] = jnp.sum(e, 0, keepdims=True)
            stat[2, i] = jnp.sum(e * gw, 0, keepdims=True)
            return carry

        lax.fori_loop(0, per_step, rows_chunk, 0)

    stack(sent_local, sent_block, sb)
    stack(own_local, own_block, wk.at[0])
    piece(0, own_block, core, 2 * core)

    loads[0].wait()
    loads[1].wait()
    pl.semaphore_wait(barrier, chips)

    def half_rows(chip):
        return pl.ds(pl.multiple_of(chip * shard + core * half, half), half)

    mine = kv.at[:, half_rows(me)]
    gathers = []
    for k in range(1, chips):
        to = lax.rem(me + k, chips)
        copy = remote(mine, mine, gat_send.at[k], gat_recv.at[me], {"prompt": to})
        copy.start()
        gathers.append(copy)
    pair_kv = remote(
        kv.at[:, own_rows], kv.at[:, own_rows], pair_send.at[0], pair_recv.at[0], partner
    )
    pair_kv.start()
    pair_q = remote(sb, wk.at[1], pair_send.at[1], pair_recv.at[1], partner)
    pair_q.start()
    pair_kv.wait_recv()
    pair_q.wait_recv()
    piece(1 - core, blocks_of[1], 0, 1)

    forwards = []
    for k in range(1, chips):
        source = lax.rem(me + chips - k, chips)
        there = kv.at[:, half_rows(source)]
        remote(there, there, gat_send.at[k], gat_recv.at[source], partner).wait_recv()
        copy = remote(there, there, fwd_send.at[k], fwd_recv.at[k], partner)
        copy.start()
        forwards.append(copy)

    piece(1, other_block, 1 - core, 2 * (1 - core))
    for copy in forwards:
        copy.wait_recv()

    slots_of = ((0,), (1, 2))
    for level in range(2):
        place = place_of[level]

        def prefix_chunk(j, carry):
            held = [slot * per_step + j for slot in slots_of[level]]
            scores = dot_nt(kv[0, :prefix_len], wk[place, 0, j])
            top = jnp.max(scores, 0, keepdims=True)
            for i in held:
                top = jnp.maximum(top, stat[0, i])
            e = jnp.exp2((scores - top) * soft)
            gw = dot_nt(kv[1, :prefix_len], wk[place, 1, j])
            total = jnp.sum(e, 0, keepdims=True)
            inner = jnp.sum(e * gw, 0, keepdims=True)
            factors = [jnp.exp2((stat[0, i] - top) * soft) for i in held]
            for i, factor in zip(held, factors):
                total = total + factor * stat[1, i]
                inner = inner + factor * stat[2, i]
            inv = 1.0 / total
            inner = inner * inv
            for i, factor in zip(held, factors):
                stat[3, i] = factor * inv
                stat[4, i] = inner
            weights = e * inv
            pt[level * per_step + j] = weights.astype(BF16)
            dt[level * per_step + j] = (weights * (gw - inner)).astype(BF16)
            return carry

        lax.fori_loop(0, per_step, prefix_chunk, 0)

    def totals(weights, grads, items):
        k_sum = v_sum = None
        for i, rows, place, j in items:
            k_part = dot_nn(grads[i, rows, :], wk[place, 0, j])
            v_part = dot_nn(weights[i, rows, :], wk[place, 1, j])
            k_sum = k_part if k_sum is None else k_sum + k_part
            v_sum = v_part if v_sum is None else v_sum + v_part
        return k_sum * scale, v_sum

    per = 256 // shard
    count = chips // per
    base = me // per + 1
    sums = []
    for n in range(count):
        chunk = lax.rem(base + n, count)
        rows = pl.ds(pl.multiple_of(chunk * 256, 256), 256)
        k_sum, v_sum = totals(
            pt,
            dt,
            [
                (level * per_step + j, rows, place_of[level], j)
                for level in range(2)
                for j in range(per_step)
            ],
        )
        span = pl.ds(chunk * per, per)
        for which, value in ((0, k_sum), (1, v_sum)):
            value = value.reshape(per, 2, half, 128)
            for c in range(2):
                tb[c, span, which] = value[:, c]
        copy = remote(tb.at[1 - core, span], rb.at[span], sum_send.at[n], sum_recv.at[n], partner)
        copy.start()
        sums.append(copy)

    def send_out(n):
        sums[n].wait_recv()
        chunk = lax.rem(base + n, count)
        span = pl.ds(chunk * per, per)
        s2[span] = (tb[core, span] + rb[span]).astype(BF16)
        for i in range(per):
            to = chunk * per + i

            @pl.when(to != me)
            def _():
                remote(
                    s2.at[to], r2.at[me], out_send.at[to], out_recv.at[me], {"prompt": to}
                ).start()

    def reply_chunk(i, carry):
        weights = er[i] * stat[3, i]
        pr[i] = weights.astype(BF16)
        dr[i] = (weights * (gr[i] - stat[4, i])).astype(BF16)
        return carry

    lax.fori_loop(0, 3 * per_step, reply_chunk, 0)
    for n in range(count):
        send_out(n)
    for c, held in ((0, ((0, 0), (1, 1))), (1, ((2, 1),))):
        rt[c, 0], rt[c, 1] = totals(
            pr,
            dr,
            [
                (slot * per_step + j, slice(None), place_of[level], j)
                for slot, level in held
                for j in range(per_step)
            ],
        )
    pair_r = remote(rt.at[1 - core], rr, pair_send.at[2], pair_recv.at[2], partner)
    pair_r.start()

    kt[...] = kv[0].astype(F32).T.astype(BF16)
    for level in range(2):
        place = place_of[level]

        def grads_chunk(j, carry):
            gq = dot_nn(kt[:, :prefix_len], dt[level * per_step + j])
            for part, slot in enumerate(slots_of[level]):
                start = prefix_len + part * own_keys
                gq += dot_nn(kt[:, start : start + own_keys], dr[slot * per_step + j])
            gq = (gq * scale).T
            for i in range(CHUNK // RBLK):
                lanes = pl.multiple_of((j * (CHUNK // RBLK) + i) * 128, 128)
                dq[place, :, pl.ds(lanes, 128)] = gq[i * RBLK : (i + 1) * RBLK]
            return carry

        lax.fori_loop(0, per_step, grads_chunk, 0)

    pair_r.wait_recv()
    rk_out[0] = rt[core, 0] + rr[0]
    rv_out[0] = rt[core, 1] + rr[1]

    total = tb[core, me] + rb[me]
    for k in range(1, chips):
        source = lax.rem(me + chips - k, chips)
        remote(
            s2.at[source], r2.at[source], out_send.at[source], out_recv.at[source], partner
        ).wait_recv()
        total = total + r2[source].astype(F32)
    pk_out[...] = total[0]
    pv_out[...] = total[1]

    for k in range(1, chips):
        to = lax.rem(me + k, chips)
        remote(s2.at[to], r2.at[me], out_send.at[to], out_recv.at[me], {"prompt": to}).wait_send()
    for copy in gathers + forwards + sums + [pair_kv, pair_q, pair_r]:
        copy.wait_send()


def finish(plan_ref, dq, pk, pv, rk, rv, dq_out, pk_out, pv_out, rk_out, rv_out, sem):
    core = lax.axis_index("resp")
    copies = []
    for s in range(dq.shape[0]):
        step = jnp.where(plan_ref[0, s] // 2 == core, 0, 1)
        rows = pl.ds(s * RBLK, RBLK)
        copies.append(pltpu.make_async_copy(dq.at[step], dq_out.at[0, rows], sem.at[s]))
    for i, (src, dst) in enumerate(((pk, pk_out), (pv, pv_out), (rk, rk_out), (rv, rv_out))):
        copies.append(pltpu.make_async_copy(src, dst, sem.at[dq.shape[0] + i]))
    for copy in copies:
        copy.start()
    for copy in copies:
        copy.wait()


def solution(mesh):
    chips = mesh.shape["prompt"]

    def local(
        queries, grad_out, keys_resp, values_resp, keys_prefix, values_prefix, lengths, block_plan
    ):
        slots, width = queries.shape[1:]
        shard, head = keys_prefix.shape
        heads = width // head
        half = shard // 2
        blocks = slots // RBLK
        own_keys = keys_resp.shape[1]
        keys = chips * shard + 2 * own_keys
        per_step = heads * RBLK // CHUNK
        count = chips // (256 // shard)
        vm = pltpu.VMEM
        dma = pltpu.SemaphoreType.DMA
        any_spec = pl.BlockSpec(memory_space=pl.ANY)
        smem = pl.BlockSpec(memory_space=pltpu.SMEM)
        vmem = pl.BlockSpec(memory_space=pltpu.VMEM)
        shapes = (
            (blocks, RBLK, width),
            (half, head),
            (half, head),
            (1, own_keys, head),
            (1, own_keys, head),
        )
        parts = pl.pallas_call(
            functools.partial(kernel, chips, heads, per_step),
            out_shape=tuple(vm(shape, F32) for shape in shapes),
            in_specs=[smem, smem] + [any_spec] * 6,
            out_specs=(vmem,) * 5,
            scratch_shapes=[
                vm((2, blocks, RBLK, width), BF16),
                vm((2, per_step, CHUNK, head), BF16),
                vm((2, 2, per_step, CHUNK, head), BF16),
                vm((2, keys, head), BF16),
                vm((head, keys), BF16),
                vm((2 * per_step, chips * shard, CHUNK), BF16),
                vm((2 * per_step, chips * shard, CHUNK), BF16),
                vm((3 * per_step, own_keys, CHUNK), BF16),
                vm((3 * per_step, own_keys, CHUNK), BF16),
                vm((3 * per_step, own_keys, CHUNK), F32),
                vm((3 * per_step, own_keys, CHUNK), F32),
                vm((5, 3 * per_step, 1, CHUNK), F32),
                vm((2, chips, 2, half, head), F32),
                vm((chips, 2, half, head), F32),
                vm((chips, 2, half, head), BF16),
                vm((chips, 2, half, head), BF16),
                vm((2, 2, own_keys, head), F32),
                vm((2, own_keys, head), F32),
                dma((6,)),
                dma((3,)),
                dma((3,)),
                dma((chips,)),
                dma((chips,)),
                dma((chips,)),
                dma((chips,)),
                dma((count,)),
                dma((count,)),
                dma((chips,)),
                dma((chips,)),
            ],
            compiler_params=pltpu.CompilerParams(
                collective_id=0, has_side_effects=True, vmem_limit_bytes=60 * 1024 * 1024
            ),
        )(
            lengths,
            block_plan,
            queries.reshape(blocks, RBLK, width),
            grad_out.reshape(blocks, RBLK, width),
            keys_resp,
            values_resp,
            keys_prefix,
            values_prefix,
        )
        parts = [pltpu.with_memory_space_constraint(part, pltpu.VMEM) for part in parts]
        shapes = ((1, slots, width),) + shapes[1:]
        return pl.pallas_call(
            finish,
            out_shape=tuple(jax.ShapeDtypeStruct(shape, F32) for shape in shapes),
            in_specs=[smem] + [vmem] * 5,
            out_specs=(any_spec,) * 5,
            scratch_shapes=[dma((blocks + 4,))],
        )(block_plan, *parts)

    placed = (
        P(("groups", "prompt"), "resp", None),
        P(("groups", "prompt"), "resp", None),
        P(("groups", "prompt"), "resp", None),
        P(("groups", "prompt"), "resp", None),
        P(("groups", "prompt"), None),
        P(("groups", "prompt"), None),
        P(("groups", "prompt")),
        P(("groups", "prompt"), "resp"),
    )
    return jax.shard_map(
        local,
        mesh=mesh,
        in_specs=placed,
        out_specs=(
            P(("groups", "prompt"), "resp", None),
            P(("groups", "prompt", "resp"), None),
            P(("groups", "prompt", "resp"), None),
            P(("groups", "prompt"), "resp", None),
            P(("groups", "prompt"), "resp", None),
        ),
        check_vma=False,
    )
```

```python
import functools
import math

import jax
import jax.numpy as jnp
from jax import lax
from jax.experimental import pallas as pl
from jax.experimental.pallas import tpu as pltpu
from jax.sharding import PartitionSpec as P

RBLK = 128
CHUNK = 256
HIDDEN = -1e30
MESH = pl.DeviceIdType.MESH
F32 = jnp.float32
BF16 = jnp.bfloat16


def remote(src, dst, send_sem, recv_sem, device):
    return pltpu.make_async_remote_copy(
        src_ref=src,
        dst_ref=dst,
        send_sem=send_sem,
        recv_sem=recv_sem,
        device_id=device,
        device_id_type=MESH,
    )


def dot_nt(a, b):
    return lax.dot_general(a, b, (((1,), (1,)), ((), ())), preferred_element_type=F32)


def dot_nn(a, b):
    return lax.dot_general(a, b, (((1,), (0,)), ((), ())), preferred_element_type=F32)


def kernel(
    chips, heads, per_step,
    len_ref, plan_ref, q_hbm, g_hbm, kr_hbm, vr_hbm, kp_hbm, vp_hbm,
    dq, pk_out, pv_out, rk_out, rv_out,
    raw, sb, wk, kv, kt, pt, dt, pr, dr, er, gr, stat, tb, rb, s2, r2, rt, rr,
    local_sem, pair_send, pair_recv, gat_send, gat_recv, fwd_send, fwd_recv,
    sum_send, sum_recv, out_send, out_recv,
):
    me = lax.axis_index("prompt")
    core = lax.axis_index("resp")
    partner = {"resp": 1 - core}
    shard = kp_hbm.shape[0]
    half = shard // 2
    prefix_len = chips * shard
    own_keys = kr_hbm.shape[1]
    reply_len = 2 * own_keys
    scale = kv.shape[2] ** (-0.5)
    soft = scale * math.log2(math.e)

    barrier = pltpu.get_barrier_semaphore()
    for k in range(1, chips):
        pl.semaphore_signal(
            barrier, inc=1, device_id={"prompt": lax.rem(me + k, chips)}, device_id_type=MESH
        )
    pl.semaphore_signal(barrier, inc=1, device_id=partner, device_id_type=MESH)

    own_rows = pl.ds(pl.multiple_of(prefix_len + core * own_keys, own_keys), own_keys)
    chip_rows = pl.ds(pl.multiple_of(me * shard, shard), shard)
    loads = [
        pltpu.make_async_copy(kp_hbm, kv.at[0, chip_rows], local_sem.at[0]),
        pltpu.make_async_copy(vp_hbm, kv.at[1, chip_rows], local_sem.at[1]),
        pltpu.make_async_copy(kr_hbm.at[0], kv.at[0, own_rows], local_sem.at[2]),
        pltpu.make_async_copy(vr_hbm.at[0], kv.at[1, own_rows], local_sem.at[3]),
        pltpu.make_async_copy(q_hbm, raw.at[0], local_sem.at[4]),
        pltpu.make_async_copy(g_hbm, raw.at[1], local_sem.at[5]),
    ]
    for load in loads:
        load.start()

    length = len_ref[0]
    first, second = plan_ref[0, 0], plan_ref[0, 1]
    own_block = jnp.where(first // 2 == core, first, second)
    other_block = jnp.where(first // 2 == core, second, first)
    own_local = lax.rem(own_block, 2)
    sent_local = 1 - own_local
    sent_block = 2 * core + sent_local

    for load in loads[2:]:
        load.wait()
    def stack(block_local, block, target):
        rows = lax.broadcasted_iota(jnp.int32, (RBLK, 128), 0) + block * RBLK
        live = rows < length
        for h in range(heads):
            lanes = slice(h * 128, (h + 1) * 128)
            place = (h * RBLK) // CHUNK
            inner = slice((h * RBLK) % CHUNK, (h * RBLK) % CHUNK + RBLK)
            target[0, place, inner, :] = raw[0, block_local, :, lanes]
            grads = raw[1, block_local, :, lanes]
            target[1, place, inner, :] = jnp.where(live, grads, jnp.zeros_like(grads))

    blocks_of = (jnp.where(core == 0, own_block, other_block), jnp.where(core == 0, other_block, own_block))
    place_of = (core, 1 - core)

    def piece(place, block, part, slot):
        keys = pl.ds(pl.multiple_of(prefix_len + part * own_keys, own_keys), own_keys)

        def rows_chunk(j, carry):
            lane = lax.broadcasted_iota(jnp.int32, (1, CHUNK), 1)
            limit = jnp.minimum(block * RBLK + lax.rem(lane, RBLK), length - 1)
            spot = lax.broadcasted_iota(jnp.int32, (own_keys, CHUNK), 0) + part * own_keys
            scores = dot_nt(kv[0, keys], wk[place, 0, j])
            scores = jnp.where(spot <= limit, scores, HIDDEN)
            top = jnp.max(scores, 0, keepdims=True)
            e = jnp.exp2((scores - top) * soft)
            gw = dot_nt(kv[1, keys], wk[place, 1, j])
            i = slot * per_step + j
            er[i] = e
            gr[i] = gw
            stat[0, i] = top
            stat[1, i] = jnp.sum(e, 0, keepdims=True)
            stat[2, i] = jnp.sum(e * gw, 0, keepdims=True)
            return carry

        lax.fori_loop(0, per_step, rows_chunk, 0, unroll=True)

    stack(sent_local, sent_block, sb)
    stack(own_local, own_block, wk.at[0])
    piece(0, own_block, core, 2 * core)

    loads[0].wait()
    loads[1].wait()
    pl.semaphore_wait(barrier, chips)

    def half_rows(chip):
        return pl.ds(pl.multiple_of(chip * shard + core * half, half), half)

    mine = kv.at[:, half_rows(me)]
    gathers = []
    for k in range(1, chips):
        to = lax.rem(me + k, chips)
        copy = remote(mine, mine, gat_send.at[k], gat_recv.at[me], {"prompt": to})
        copy.start()
        gathers.append(copy)
    pair_kv = remote(
        kv.at[:, own_rows], kv.at[:, own_rows], pair_send.at[0], pair_recv.at[0], partner
    )
    pair_kv.start()
    pair_q = remote(sb, wk.at[1], pair_send.at[1], pair_recv.at[1], partner)
    pair_q.start()
    pair_kv.wait_recv()
    pair_q.wait_recv()
    piece(1 - core, blocks_of[1], 0, 1)

    forwards = []
    for k in range(1, chips):
        source = lax.rem(me + chips - k, chips)
        there = kv.at[:, half_rows(source)]
        remote(there, there, gat_send.at[k], gat_recv.at[source], partner).wait_recv()
        copy = remote(there, there, fwd_send.at[k], fwd_recv.at[k], partner)
        copy.start()
        forwards.append(copy)

    piece(1, other_block, 1 - core, 2 * (1 - core))
    for copy in forwards:
        copy.wait_recv()

    slots_of = ((0,), (1, 2))
    for level in range(2):
        place = place_of[level]

        def prefix_chunk(j, carry):
            held = [slot * per_step + j for slot in slots_of[level]]
            scores = dot_nt(kv[0, :prefix_len], wk[place, 0, j])
            top = jnp.max(scores, 0, keepdims=True)
            for i in held:
                top = jnp.maximum(top, stat[0, i])
            e = jnp.exp2((scores - top) * soft)
            gw = dot_nt(kv[1, :prefix_len], wk[place, 1, j])
            total = jnp.sum(e, 0, keepdims=True)
            inner = jnp.sum(e * gw, 0, keepdims=True)
            factors = [jnp.exp2((stat[0, i] - top) * soft) for i in held]
            for i, factor in zip(held, factors):
                total = total + factor * stat[1, i]
                inner = inner + factor * stat[2, i]
            inv = 1.0 / total
            inner = inner * inv
            for i, factor in zip(held, factors):
                stat[3, i] = factor * inv
                stat[4, i] = inner
            weights = e * inv
            pt[level * per_step + j] = weights.astype(BF16)
            dt[level * per_step + j] = (weights * (gw - inner)).astype(BF16)
            return carry

        lax.fori_loop(0, per_step, prefix_chunk, 0, unroll=True)

    def totals(weights, grads, items):
        k_sum = v_sum = None
        for i, rows, place, j in items:
            k_part = dot_nn(grads[i, rows, :], wk[place, 0, j])
            v_part = dot_nn(weights[i, rows, :], wk[place, 1, j])
            k_sum = k_part if k_sum is None else k_sum + k_part
            v_sum = v_part if v_sum is None else v_sum + v_part
        return k_sum * scale, v_sum

    per = 256 // shard
    count = chips // per
    base = me // per + 1
    sums = []
    for n in range(count):
        chunk = lax.rem(base + n, count)
        rows = pl.ds(pl.multiple_of(chunk * 256, 256), 256)
        k_sum, v_sum = totals(
            pt,
            dt,
            [
                (level * per_step + j, rows, place_of[level], j)
                for level in range(2)
                for j in range(per_step)
            ],
        )
        span = pl.ds(chunk * per, per)
        for which, value in ((0, k_sum), (1, v_sum)):
            value = value.reshape(per, 2, half, 128)
            for c in range(2):
                tb[c, span, which] = value[:, c]
        copy = remote(tb.at[1 - core, span], rb.at[span], sum_send.at[n], sum_recv.at[n], partner)
        copy.start()
        sums.append(copy)

    def send_out(n):
        sums[n].wait_recv()
        chunk = lax.rem(base + n, count)
        span = pl.ds(chunk * per, per)
        s2[span] = (tb[core, span] + rb[span]).astype(BF16)
        for i in range(per):
            to = chunk * per + i

            @pl.when(to != me)
            def _():
                remote(
                    s2.at[to], r2.at[me], out_send.at[to], out_recv.at[me], {"prompt": to}
                ).start()

    def reply_chunk(i, carry):
        weights = er[i] * stat[3, i]
        pr[i] = weights.astype(BF16)
        dr[i] = (weights * (gr[i] - stat[4, i])).astype(BF16)
        return carry

    lax.fori_loop(0, 3 * per_step, reply_chunk, 0, unroll=per_step)
    for n in range(count):
        send_out(n)
    for c, held in ((0, ((0, 0), (1, 1))), (1, ((2, 1),))):
        rt[c, 0], rt[c, 1] = totals(
            pr,
            dr,
            [
                (slot * per_step + j, slice(None), place_of[level], j)
                for slot, level in held
                for j in range(per_step)
            ],
        )
    pair_r = remote(rt.at[1 - core], rr, pair_send.at[2], pair_recv.at[2], partner)
    pair_r.start()

    kt[...] = kv[0].astype(F32).T.astype(BF16)
    for level in range(2):
        place = place_of[level]

        def grads_chunk(j, carry):
            gq = dot_nn(kt[:, :prefix_len], dt[level * per_step + j])
            for part, slot in enumerate(slots_of[level]):
                start = prefix_len + part * own_keys
                gq += dot_nn(kt[:, start : start + own_keys], dr[slot * per_step + j])
            gq = (gq * scale).T
            for i in range(CHUNK // RBLK):
                lanes = pl.multiple_of((j * (CHUNK // RBLK) + i) * 128, 128)
                dq[place, :, pl.ds(lanes, 128)] = gq[i * RBLK : (i + 1) * RBLK]
            return carry

        lax.fori_loop(0, per_step, grads_chunk, 0, unroll=True)

    pair_r.wait_recv()
    rk_out[0] = rt[core, 0] + rr[0]
    rv_out[0] = rt[core, 1] + rr[1]

    total = tb[core, me] + rb[me]
    for k in range(1, chips):
        source = lax.rem(me + chips - k, chips)
        remote(
            s2.at[source], r2.at[source], out_send.at[source], out_recv.at[source], partner
        ).wait_recv()
        total = total + r2[source].astype(F32)
    pk_out[...] = total[0]
    pv_out[...] = total[1]

    for k in range(1, chips):
        to = lax.rem(me + k, chips)
        remote(s2.at[to], r2.at[me], out_send.at[to], out_recv.at[me], {"prompt": to}).wait_send()
    for copy in gathers + forwards + sums + [pair_kv, pair_q, pair_r]:
        copy.wait_send()


def finish(plan_ref, dq, pk, pv, rk, rv, dq_out, pk_out, pv_out, rk_out, rv_out, sem):
    core = lax.axis_index("resp")
    copies = []
    for s in range(dq.shape[0]):
        step = jnp.where(plan_ref[0, s] // 2 == core, 0, 1)
        rows = pl.ds(s * RBLK, RBLK)
        copies.append(pltpu.make_async_copy(dq.at[step], dq_out.at[0, rows], sem.at[s]))
    for i, (src, dst) in enumerate(((pk, pk_out), (pv, pv_out), (rk, rk_out), (rv, rv_out))):
        copies.append(pltpu.make_async_copy(src, dst, sem.at[dq.shape[0] + i]))
    for copy in copies:
        copy.start()
    for copy in copies:
        copy.wait()


def solution(mesh):
    chips = mesh.shape["prompt"]

    def local(
        queries, grad_out, keys_resp, values_resp, keys_prefix, values_prefix, lengths, block_plan
    ):
        slots, width = queries.shape[1:]
        shard, head = keys_prefix.shape
        heads = width // head
        half = shard // 2
        blocks = slots // RBLK
        own_keys = keys_resp.shape[1]
        keys = chips * shard + 2 * own_keys
        per_step = heads * RBLK // CHUNK
        count = chips // (256 // shard)
        vm = pltpu.VMEM
        dma = pltpu.SemaphoreType.DMA
        any_spec = pl.BlockSpec(memory_space=pl.ANY)
        smem = pl.BlockSpec(memory_space=pltpu.SMEM)
        vmem = pl.BlockSpec(memory_space=pltpu.VMEM)
        shapes = (
            (blocks, RBLK, width),
            (half, head),
            (half, head),
            (1, own_keys, head),
            (1, own_keys, head),
        )
        parts = pl.pallas_call(
            functools.partial(kernel, chips, heads, per_step),
            out_shape=tuple(vm(shape, F32) for shape in shapes),
            in_specs=[smem, smem] + [any_spec] * 6,
            out_specs=(vmem,) * 5,
            scratch_shapes=[
                vm((2, blocks, RBLK, width), BF16),
                vm((2, per_step, CHUNK, head), BF16),
                vm((2, 2, per_step, CHUNK, head), BF16),
                vm((2, keys, head), BF16),
                vm((head, keys), BF16),
                vm((2 * per_step, chips * shard, CHUNK), BF16),
                vm((2 * per_step, chips * shard, CHUNK), BF16),
                vm((3 * per_step, own_keys, CHUNK), BF16),
                vm((3 * per_step, own_keys, CHUNK), BF16),
                vm((3 * per_step, own_keys, CHUNK), F32),
                vm((3 * per_step, own_keys, CHUNK), F32),
                vm((5, 3 * per_step, 1, CHUNK), F32),
                vm((2, chips, 2, half, head), F32),
                vm((chips, 2, half, head), F32),
                vm((chips, 2, half, head), BF16),
                vm((chips, 2, half, head), BF16),
                vm((2, 2, own_keys, head), F32),
                vm((2, own_keys, head), F32),
                dma((6,)),
                dma((3,)),
                dma((3,)),
                dma((chips,)),
                dma((chips,)),
                dma((chips,)),
                dma((chips,)),
                dma((count,)),
                dma((count,)),
                dma((chips,)),
                dma((chips,)),
            ],
            compiler_params=pltpu.CompilerParams(
                collective_id=0, has_side_effects=True, vmem_limit_bytes=60 * 1024 * 1024
            ),
        )(
            lengths,
            block_plan,
            queries.reshape(blocks, RBLK, width),
            grad_out.reshape(blocks, RBLK, width),
            keys_resp,
            values_resp,
            keys_prefix,
            values_prefix,
        )
        parts = [pltpu.with_memory_space_constraint(part, pltpu.VMEM) for part in parts]
        shapes = ((1, slots, width),) + shapes[1:]
        return pl.pallas_call(
            finish,
            out_shape=tuple(jax.ShapeDtypeStruct(shape, F32) for shape in shapes),
            in_specs=[smem] + [vmem] * 5,
            out_specs=(any_spec,) * 5,
            scratch_shapes=[dma((blocks + 4,))],
        )(block_plan, *parts)

    placed = (
        P(("groups", "prompt"), "resp", None),
        P(("groups", "prompt"), "resp", None),
        P(("groups", "prompt"), "resp", None),
        P(("groups", "prompt"), "resp", None),
        P(("groups", "prompt"), None),
        P(("groups", "prompt"), None),
        P(("groups", "prompt")),
        P(("groups", "prompt"), "resp"),
    )
    return jax.shard_map(
        local,
        mesh=mesh,
        in_specs=placed,
        out_specs=(
            P(("groups", "prompt"), "resp", None),
            P(("groups", "prompt", "resp"), None),
            P(("groups", "prompt", "resp"), None),
            P(("groups", "prompt"), "resp", None),
            P(("groups", "prompt"), "resp", None),
        ),
        check_vma=False,
    )
```
